32 devices in a mesh: ctx: 8 (over z, x), tp: 4 (over y, core).
Axes of the slice: x: 2, y: 2, z: 4, core: 2. Of those that a mesh axis runs over, the one named last changes fastest.
Arguments:
- q_nope: bfloat16 [8, 128, 128], P('ctx', 'tp'), may hold values from -6 to 6
- q_rope: bfloat16 [8, 128, 64], P('ctx', 'tp'), may hold values from -256 to 256
- w_uk: bfloat16 [128, 128, 512], P('tp'), may hold values from -0.5 to 0.5
- w_uv: bfloat16 [128, 512, 128], P('tp'), may hold values from -3 to 3
- w_out: bfloat16 [16384, 7168], P('tp', 'ctx'), may hold values from -0.046875 to 0.046875
- prefix_cache: bfloat16 [32768, 576], P('ctx'), may hold values from -6 to 6
- block_table: int32 [512], P('ctx'), may hold values from 0 to 511, each once
- prefix_len: int32 [8], replicated, may hold values from 8192 to 32768
- suffix_cache: bfloat16 [8, 256, 576], P('ctx'), may hold values from -12 to 12
- suffix_len: int32 [8], P('ctx'), may hold values from 2 to 256
Outputs:
- layer_out: bfloat16 [8, 7168], P('tp', 'ctx')
The draws below stay inside these ranges and needn't reach their ends.
Inputs may be any that keep to these rules, and one draw needn't show every extreme that they name: A permutation: slots b * 64 to b * 64 + 63 of prefix_cache hold prefix positions block_table[b] * 64 onwards.
All inputs are finite; a program needn't handle non-finite values.
Results may differ from the reference program's by a relative error of at most 0.0078.
Values may be sent and summed in bfloat16 or wider, within the bound.
A program may use at most 64 MiB of HBM per device.

```python
import jax
import jax.numpy as jnp
from jax import lax

H = 128
LAT = 512
ROPE = 64
NOPE = 128
VDIM = 128
D = 7168
TOK_DEV = 4096
BLOCK = 64
SUF = 256
REQUESTS = 8
NPRE = 32768
NBLK = 512
N_CTX = 8


def shared_base(key):
    return jax.random.normal(jax.random.fold_in(key, 11), (REQUESTS, ROPE), jnp.float32)


def suffix_rope_part(key):
    noise = jax.random.normal(jax.random.fold_in(key, 13), (REQUESTS, SUF, ROPE), jnp.float32)
    return shared_base(key)[:, None, :] + noise


def draw_suffix_cache(key, part):
    latent = jax.random.normal(jax.random.fold_in(key, 12), (REQUESTS, SUF, LAT), jnp.float32)
    rope = suffix_rope_part(key)
    return jnp.clip(jnp.concatenate([latent, rope], axis=2), -12.0, 12.0).astype(jnp.bfloat16)


def draw_q_rope(key, part):
    noise = jax.random.normal(jax.random.fold_in(key, 21), (REQUESTS, H, ROPE), jnp.float32)
    query = shared_base(key)[:, None, :] + noise
    return jnp.clip(query, -256.0, 256.0).astype(jnp.bfloat16)


def set_ends(drawn, stream_key, low, top_value):
    longest = drawn.shape.index(max(drawn.shape))
    spots = []
    for shift in (0, 1):
        where = [jax.random.randint(jax.random.fold_in(stream_key, axis), (), 0, length) for axis, length in enumerate(drawn.shape)]
        where[longest] = (where[longest] + shift) % drawn.shape[longest]
        spots.append(tuple(where))
    return drawn.at[spots[0]].set(low).at[spots[1]].set(top_value)


def block_scale(stream_key, dims, split, low, high):
    def one(axis_at, blocks):
        steps = jax.random.uniform(jax.random.fold_in(jax.random.fold_in(stream_key, 6), axis_at), (blocks,), jnp.float32, low / len(split), high / len(split))
        return jnp.repeat(jnp.exp(steps), dims[axis_at] // blocks).reshape((-1,) + (1,) * (len(dims) - axis_at - 1))

    level = one(*split[0])
    for cut in split[1:]:
        level = level * one(*cut)
    return level


def normal_values(own_key, shape, scale, bound, split=(), held_as=jnp.bfloat16):
    entries = scale * jax.random.normal(own_key, shape, jnp.float32)
    if split:
        entries = entries * block_scale(own_key, shape, split, -0.22, 0.18)
    return jnp.clip(entries, -bound, bound).astype(held_as)


def setup_inputs(seed: int = 0) -> dict:
    streams_of = jax.random.split(jax.random.key(seed), 11)
    q_nope = normal_values(streams_of[0], (REQUESTS, H, NOPE), 1.0, 6.0, ((0, 8), (1, 4)))
    q_rope = draw_q_rope(jax.random.fold_in(streams_of[10], 71), 0)
    w_uk = normal_values(streams_of[2], (H, NOPE, LAT), NOPE ** -0.5, 0.5, ((0, 4),))
    w_uv = normal_values(streams_of[3], (H, LAT, VDIM), 0.5, 3.0, ((0, 4),))
    w_out = normal_values(streams_of[4], (H * VDIM, D), (H * VDIM) ** -0.5, 0.046875, ((0, 4), (1, 8)))
    prefix_cache = normal_values(streams_of[5], (NPRE, LAT + ROPE), 1.0, 6.0, ((0, 8),))
    block_table = jax.random.permutation(streams_of[6], NBLK).astype(jnp.int32)
    prefix_len = set_ends(jax.random.randint(streams_of[7], (REQUESTS,), NPRE // 4, NPRE + 1), jax.random.fold_in(streams_of[7], 1), NPRE // 4, NPRE).astype(jnp.int32)
    suffix_cache = draw_suffix_cache(jax.random.fold_in(streams_of[10], 71), 0)
    suffix_len = set_ends(jax.random.randint(streams_of[9], (REQUESTS,), 2, SUF + 1), jax.random.fold_in(streams_of[9], 1), 2, SUF).astype(jnp.int32)
    return {"q_nope": q_nope, "q_rope": q_rope, "w_uk": w_uk, "w_uv": w_uv, "w_out": w_out, "prefix_cache": prefix_cache, "block_table": block_table, "prefix_len": prefix_len, "suffix_cache": suffix_cache, "suffix_len": suffix_len}


masked_value = -1e30


def summarize(scores, visible, values, pattern):
    row_peak = jnp.max(jnp.where(visible, scores, masked_value), axis=2)
    weights = jnp.where(visible, jnp.exp(scores - row_peak[:, :, None]), 0.0).astype(jnp.bfloat16)
    weights = lax.optimization_barrier(weights).astype(jnp.float32)
    return row_peak, jnp.sum(weights, axis=2), jnp.einsum(pattern, weights, values)


def reference(q_nope, q_rope, w_uk, w_uv, w_out, prefix_cache, block_table, prefix_len, suffix_cache, suffix_len):
    softmax_scale = (NOPE + ROPE) ** -0.5
    q_latent = jnp.einsum("rhn,hnc->rhc", q_nope.astype(jnp.float32), w_uk.astype(jnp.float32)).astype(jnp.bfloat16)
    joined = lax.optimization_barrier(jnp.concatenate([q_latent, q_rope], axis=2)).astype(jnp.float32)
    positions = (block_table[:, None] * BLOCK + jnp.arange(BLOCK, dtype=jnp.int32)[None, :]).reshape(N_CTX, TOK_DEV)
    segments = prefix_cache.reshape(N_CTX, TOK_DEV, LAT + ROPE)

    def segment_part(pieces):
        block_cache, block_positions = pieces
        cache_wide = block_cache.astype(jnp.float32)
        scores = jnp.einsum("rhc,tc->rht", joined, cache_wide) * softmax_scale
        visible = (block_positions[None, :] < prefix_len[:, None])[:, None, :]
        return summarize(scores, visible, cache_wide[:, :LAT], "rht,tc->rhc")

    seg_peak, seg_mass, seg_weighted = lax.map(segment_part, (segments, positions))
    suffix_wide = suffix_cache.astype(jnp.float32)
    suffix_scores = jnp.einsum("rhc,rtc->rht", joined, suffix_wide) * softmax_scale
    suffix_slots = jnp.arange(SUF, dtype=jnp.int32)
    suffix_visible = (suffix_slots[None, :] < suffix_len[:, None])[:, None, :]
    tail_peak, tail_mass, tail_weighted = summarize(suffix_scores, suffix_visible, suffix_wide[:, :, :LAT], "rht,rtc->rhc")
    highest = jnp.maximum(jnp.max(seg_peak, axis=0), tail_peak)
    factors = jnp.exp(seg_peak - highest[None])
    tail_factor = jnp.exp(tail_peak - highest)
    total_mass = jnp.sum(factors * seg_mass, axis=0) + tail_factor * tail_mass
    total_weighted = jnp.sum(factors[..., None] * seg_weighted, axis=0) + tail_factor[:, :, None] * tail_weighted
    attention = total_weighted / total_mass[:, :, None]
    head_values = jnp.einsum("rhc,hcv->rhv", attention, w_uv.astype(jnp.float32), precision=lax.Precision.HIGHEST).astype(jnp.bfloat16)
    flat_values = head_values.reshape(REQUESTS, H * VDIM)
    return jnp.dot(flat_values, w_out, preferred_element_type=jnp.float32).astype(jnp.bfloat16)
```

```python
import functools

import jax
import jax.numpy as jnp
from jax import lax
from jax.experimental import pallas as pl
from jax.experimental.pallas import tpu as pltpu
from jax.sharding import PartitionSpec as P

LAT = 512
ROPE = 64
NOPE = 128
BLOCK = 64
LANES = 128
MASKED = -1e30
FLOOR = -1e29
LOG2E = 1.4426950408889634
MESH = pl.DeviceIdType.MESH


def thirds(x):
    a = x.astype(jnp.bfloat16).astype(jnp.float32)
    rest = x - a
    b = rest.astype(jnp.bfloat16).astype(jnp.float32)
    return a, b, (rest - b).astype(jnp.bfloat16).astype(jnp.float32)


def kernel(
    sizes,
    table_ref,
    prefix_len_ref,
    suffix_len_ref,
    q_nope_ref,
    q_rope_ref,
    w_uk_hbm,
    w_uv_hbm,
    w_out_hbm,
    prefix_hbm,
    suffix_hbm,
    out_ref,
    qn_all,
    qr_all,
    qn_rows,
    query,
    w_uk,
    w_uv,
    w_out,
    cache,
    mask,
    scores,
    peak,
    mass,
    weighted,
    msg,
    got,
    hv_all,
    part,
    part_got,
    load_sem,
    q_send,
    q_recv,
    m_send,
    m_recv,
    h_send,
    h_recv,
    p_send,
    p_recv,
):
    n, t, own, heads, requests, tokens, suffix, chunk = sizes
    rows = requests * heads
    block_rows = rows // n
    block_heads = max(1, block_rows // requests)
    head_rows = min(block_rows, requests)
    vdim = w_uv.shape[2]
    me = lax.axis_index("ctx")
    me_tp = lax.axis_index("tp")
    chunks = tokens // chunk

    loads = [pltpu.make_async_copy(w_uk_hbm, w_uk, load_sem.at[0])]
    for c in range(chunks):
        part_of = pl.ds(c * chunk, chunk)
        loads.append(
            pltpu.make_async_copy(prefix_hbm.at[part_of], cache.at[part_of], load_sem.at[1 + c])
        )
    for o in range(own):
        loads.append(
            pltpu.make_async_copy(
                suffix_hbm.at[o],
                cache.at[pl.ds(tokens + o * suffix, suffix)],
                load_sem.at[1 + chunks + o],
            )
        )
    first_head = (me * block_rows) // requests
    uv_load = pltpu.make_async_copy(
        w_uv_hbm.at[pl.ds(first_head, block_heads)], w_uv, load_sem.at[1 + chunks + own]
    )
    out_load = pltpu.make_async_copy(w_out_hbm, w_out, load_sem.at[2 + chunks + own])
    for load in loads:
        load.start()
    uv_load.start()
    out_load.start()

    barrier = pltpu.get_barrier_semaphore()
    for k in range(1, n):
        pl.semaphore_signal(
            barrier, inc=1, device_id=(lax.rem(me + k, n), me_tp), device_id_type=MESH
        )
    for k in range(1, t):
        pl.semaphore_signal(
            barrier, inc=1, device_id=(me, lax.rem(me_tp + k, t)), device_id_type=MESH
        )
    pl.semaphore_wait(barrier, n - 1 + t - 1)

    q_copies = []
    for k in range(1, n):
        to = (lax.rem(me + k, n), me_tp)
        for i, (src, dst) in enumerate(((q_nope_ref, qn_all), (q_rope_ref, qr_all))):
            copy = pltpu.make_async_remote_copy(
                src_ref=src,
                dst_ref=dst.at[pl.ds(me * own, own)],
                send_sem=q_send.at[i, k],
                recv_sem=q_recv.at[i, k],
                device_id=to,
                device_id_type=MESH,
            )
            copy.start()
            q_copies.append(copy)
    qn_all[pl.ds(me * own, own)] = q_nope_ref[...]
    qr_all[pl.ds(me * own, own)] = q_rope_ref[...]

    row = lax.broadcasted_iota(jnp.int32, (requests, LANES), 0)
    lane = lax.broadcasted_iota(jnp.int32, (requests, LANES), 1)
    limit = jnp.zeros((requests, LANES), jnp.int32)
    for r in range(requests):
        limit = jnp.where(row == r, prefix_len_ref[r], limit)
    per_tile = LANES // BLOCK
    for i in range(tokens // LANES):
        position = lane + table_ref[i * per_tile] * BLOCK
        for j in range(1, per_tile):
            moved = lane + (table_ref[i * per_tile + j] * BLOCK - j * BLOCK)
            position = jnp.where(lane >= j * BLOCK, moved, position)
        mask[:, i * LANES : (i + 1) * LANES] = jnp.where(position < limit, 0.0, MASKED)
    for o in range(own):
        for i in range(suffix // LANES):
            slot = lane + i * LANES
            start = tokens + o * suffix + i * LANES
            seen = (slot < suffix_len_ref[o]) & (row == me * own + o)
            mask[:, start : start + LANES] = jnp.where(seen, 0.0, MASKED)

    to_row = lax.broadcasted_iota(jnp.int32, (rows, rows), 0)
    from_row = lax.broadcasted_iota(jnp.int32, (rows, rows), 1)
    wanted = (to_row % requests) * heads + to_row // requests
    shuffle = jnp.where(from_row == wanted, 1.0, 0.0).astype(jnp.bfloat16)
    for copy in q_copies:
        copy.wait()
    qn_rows[...] = jnp.dot(
        shuffle, qn_all[...].reshape(rows, NOPE), preferred_element_type=jnp.float32
    )
    query[:, LAT:] = jnp.dot(
        shuffle, qr_all[...].reshape(rows, ROPE), preferred_element_type=jnp.float32
    ).astype(jnp.bfloat16)
    loads[0].wait()
    group = 8

    def absorb(g, carry):
        latents = []
        for j in range(group):
            h = g * group + j
            q = qn_rows[pl.ds(pl.multiple_of(h * requests, requests), requests), :]
            latents.append(
                jnp.dot(q.astype(jnp.bfloat16), w_uk[h], preferred_element_type=jnp.float32)
            )
        at = pl.multiple_of(g * (group * requests), group * requests)
        query[pl.ds(at, group * requests), :LAT] = jnp.concatenate(latents, axis=0).astype(
            jnp.bfloat16
        )
        return carry

    lax.fori_loop(0, heads // group, absorb, 0)

    scale = LOG2E * (NOPE + ROPE) ** (-0.5)
    spans = [(c * chunk, chunk) for c in range(chunks)]
    spans += [(tokens + o * suffix, suffix) for o in range(own)]
    for i, (start, length) in enumerate(spans):
        loads[1 + i].wait()
        s = lax.dot_general(
            query[...],
            cache[start : start + length, :],
            (((1,), (1,)), ((), ())),
            preferred_element_type=jnp.float32,
        )
        s = (s * scale).reshape(heads, requests, length) + mask[:, start : start + length][None]
        s = s.reshape(rows, length)
        scores[:, start : start + length] = s
        top = s[:, :LANES]
        for j in range(1, length // LANES):
            top = jnp.maximum(top, s[:, j * LANES : (j + 1) * LANES])
        peak[...] = top if i == 0 else jnp.maximum(peak[...], top)
    highest = jnp.maximum(jnp.max(peak[...], axis=1, keepdims=True), FLOOR)
    peak[...] = jnp.broadcast_to(highest, (rows, LANES))
    for i, (start, length) in enumerate(spans):
        p = jnp.exp2(scores[:, start : start + length] - peak[:, :1]).astype(jnp.bfloat16)
        wide = p.astype(jnp.float32)
        total = wide[:, :LANES]
        for j in range(1, length // LANES):
            total = total + wide[:, j * LANES : (j + 1) * LANES]
        mass[...] = total if i == 0 else mass[...] + total
        term = jnp.dot(
            p, cache[start : start + length, :LAT], preferred_element_type=jnp.float32
        )
        weighted[...] = term if i == 0 else weighted[...] + term

    sums = jnp.sum(mass[...], axis=1, keepdims=True)
    at_lane = lax.broadcasted_iota(jnp.int32, (rows, LANES), 1)
    stats = jnp.zeros((rows, LANES), jnp.float32)
    for i, piece in enumerate(thirds(peak[:, :1]) + thirds(sums)):
        stats = jnp.where(at_lane == i, piece, stats)
    msg[:, :, :LAT] = weighted[...].astype(jnp.bfloat16).reshape(n, block_rows, LAT)
    msg[:, :, LAT:] = stats.astype(jnp.bfloat16).reshape(n, block_rows, LANES)
    m_copies = []
    for k in range(1, n):
        to = lax.rem(me + k, n)
        copy = pltpu.make_async_remote_copy(
            src_ref=msg.at[to],
            dst_ref=got.at[k],
            send_sem=m_send.at[k],
            recv_sem=m_recv.at[k],
            device_id=(to, me_tp),
            device_id_type=MESH,
        )
        copy.start()
        m_copies.append(copy)
    got[0] = msg[me]
    uv_load.wait()
    for copy in m_copies:
        copy.wait()

    tops, totals = [], []
    for k in range(n):
        stat = got[k, :, LAT:].astype(jnp.float32)
        tops.append(stat[:, 0:1] + stat[:, 1:2] + stat[:, 2:3])
        totals.append(stat[:, 3:4] + stat[:, 4:5] + stat[:, 5:6])
    best = functools.reduce(jnp.maximum, tops)
    factors = [jnp.exp2(top - best) for top in tops]
    whole = sum(f * m for f, m in zip(factors, totals))
    latent = sum(f * got[k, :, :LAT].astype(jnp.float32) for k, f in enumerate(factors)) / whole
    values = []
    for j in range(block_heads):
        pieces = jnp.concatenate(thirds(latent[j * head_rows : (j + 1) * head_rows]), axis=0)
        y = jnp.dot(pieces.astype(jnp.bfloat16), w_uv[j], preferred_element_type=jnp.float32)
        values.append(y[:head_rows] + y[head_rows : 2 * head_rows] + y[2 * head_rows :])
    hv_all[me] = jnp.concatenate(values, axis=1).astype(jnp.bfloat16)
    h_copies = []
    for k in range(1, n):
        copy = pltpu.make_async_remote_copy(
            src_ref=hv_all.at[me],
            dst_ref=hv_all.at[me],
            send_sem=h_send.at[k],
            recv_sem=h_recv.at[k],
            device_id=(lax.rem(me + k, n), me_tp),
            device_id_type=MESH,
        )
        copy.start()
        h_copies.append(copy)
    out_load.wait()

    if block_rows >= requests:
        depth = block_heads * vdim
        total = None
        for k in range(n):
            source = lax.rem(me + n - k, n)
            if k:
                h_copies[k - 1].wait_recv()
            term = jnp.dot(
                hv_all[source],
                w_out[pl.ds(pl.multiple_of(source * depth, depth), depth), :],
                preferred_element_type=jnp.float32,
            )
            total = term if k == 0 else total + term
    else:
        for copy in h_copies:
            copy.wait_recv()
        split = requests // block_rows
        total = None
        for h in range(heads):
            lhs = jnp.concatenate([hv_all[h * split + i] for i in range(split)], axis=0)
            term = jnp.dot(
                lhs, w_out[h * vdim : (h + 1) * vdim, :], preferred_element_type=jnp.float32
            )
            total = term if h == 0 else total + term
    for copy in h_copies:
        copy.wait_send()

    share = requests // t
    for i in range(t):
        part[i] = total[i * share : (i + 1) * share]
    p_copies = []
    for k in range(1, t):
        to = lax.rem(me_tp + k, t)
        copy = pltpu.make_async_remote_copy(
            src_ref=part.at[to],
            dst_ref=part_got.at[k],
            send_sem=p_send.at[k],
            recv_sem=p_recv.at[k],
            device_id=(me, to),
            device_id_type=MESH,
        )
        copy.start()
        p_copies.append(copy)
    result = part[me_tp]
    for k in range(1, t):
        p_copies[k - 1].wait()
        result = result + part_got[k]
    out_ref[...] = result.astype(jnp.bfloat16)


def on_device(
    n,
    t,
    q_nope,
    q_rope,
    w_uk,
    w_uv,
    w_out,
    prefix_cache,
    block_table,
    prefix_len,
    suffix_cache,
    suffix_len,
):
    own, heads, _ = q_nope.shape
    requests = own * n
    tokens, width = prefix_cache.shape
    suffix = suffix_cache.shape[1]
    chunk = 1024 if tokens % 1024 == 0 else tokens
    chunks = tokens // chunk
    slots = tokens + own * suffix
    rows = requests * heads
    block_rows = rows // n
    block_heads = max(1, block_rows // requests)
    head_rows = min(block_rows, requests)
    vdim = w_uv.shape[2]
    columns = w_out.shape[1]
    share = requests // t
    bf, f32 = jnp.bfloat16, jnp.float32
    sizes = (n, t, own, heads, requests, tokens, suffix, chunk)
    smem = pl.BlockSpec(memory_space=pltpu.SMEM)
    vmem = pl.BlockSpec(memory_space=pltpu.VMEM)
    hbm = pl.BlockSpec(memory_space=pl.ANY)
    dma = pltpu.SemaphoreType.DMA
    return pl.pallas_call(
        functools.partial(kernel, sizes),
        out_shape=jax.ShapeDtypeStruct((share, columns), bf),
        in_specs=[smem] * 3 + [vmem] * 2 + [hbm] * 5,
        out_specs=vmem,
        scratch_shapes=[
            pltpu.VMEM((requests, heads, NOPE), bf),
            pltpu.VMEM((requests, heads, ROPE), bf),
            pltpu.VMEM((rows, NOPE), f32),
            pltpu.VMEM((rows, width), bf),
            pltpu.VMEM(w_uk.shape, bf),
            pltpu.VMEM((block_heads,) + w_uv.shape[1:], bf),
            pltpu.VMEM(w_out.shape, bf),
            pltpu.VMEM((slots, width), bf),
            pltpu.VMEM((requests, slots), f32),
            pltpu.VMEM((rows, slots), f32),
            pltpu.VMEM((rows, LANES), f32),
            pltpu.VMEM((rows, LANES), f32),
            pltpu.VMEM((rows, LAT), f32),
            pltpu.VMEM((n, block_rows, LAT + LANES), bf),
            pltpu.VMEM((n, block_rows, LAT + LANES), bf),
            pltpu.VMEM((n, head_rows, block_heads * vdim), bf),
            pltpu.VMEM((t, share, columns), f32),
            pltpu.VMEM((t, share, columns), f32),
            dma((3 + chunks + own,)),
            dma((2, n)),
            dma((2, n)),
            dma((n,)),
            dma((n,)),
            dma((n,)),
            dma((n,)),
            dma((t,)),
            dma((t,)),
        ],
        compiler_params=pltpu.CompilerParams(
            collective_id=0, has_side_effects=True, vmem_limit_bytes=60 * 1024 * 1024
        ),
    )(
        block_table,
        prefix_len,
        suffix_len,
        q_nope,
        q_rope,
        w_uk,
        w_uv,
        w_out,
        prefix_cache,
        suffix_cache,
    )


def solution(mesh):
    placed = (
        P("ctx", "tp", None),
        P("ctx", "tp", None),
        P("tp", None, None),
        P("tp", None, None),
        P("tp", "ctx"),
        P("ctx", None),
        P("ctx"),
        P(),
        P("ctx", None, None),
        P("ctx"),
    )
    return jax.shard_map(
        functools.partial(on_device, mesh.shape["ctx"], mesh.shape["tp"]),
        mesh=mesh,
        in_specs=placed,
        out_specs=P("tp", "ctx"),
        check_vma=False,
    )
```

```python
import functools

import jax
import jax.numpy as jnp
from jax import lax
from jax.experimental import pallas as pl
from jax.experimental.pallas import tpu as pltpu
from jax.sharding import PartitionSpec as P

LAT = 512
ROPE = 64
NOPE = 128
BLOCK = 64
LANES = 128
MASKED = -1e30
FLOOR = -1e29
LOG2E = 1.4426950408889634
MESH = pl.DeviceIdType.MESH


def thirds(x):
    a = x.astype(jnp.bfloat16).astype(jnp.float32)
    rest = x - a
    b = rest.astype(jnp.bfloat16).astype(jnp.float32)
    return a, b, (rest - b).astype(jnp.bfloat16).astype(jnp.float32)


def kernel(
    sizes,
    table_ref,
    prefix_len_ref,
    suffix_len_ref,
    q_nope_ref,
    q_rope_ref,
    w_uk_hbm,
    w_uv_hbm,
    w_out_hbm,
    prefix_hbm,
    suffix_hbm,
    out_ref,
    qn_all,
    qr_all,
    qn_rows,
    query,
    w_uk,
    w_uv,
    w_out,
    cache,
    mask,
    scores,
    peak,
    mass,
    weighted,
    msg,
    got,
    hv_all,
    part,
    part_got,
    load_sem,
    q_send,
    q_recv,
    m_send,
    m_recv,
    h_send,
    h_recv,
    p_send,
    p_recv,
):
    n, t, own, heads, requests, tokens, suffix, chunk = sizes
    rows = requests * heads
    block_rows = rows // n
    block_heads = max(1, block_rows // requests)
    head_rows = min(block_rows, requests)
    vdim = w_uv.shape[2]
    me = lax.axis_index("ctx")
    me_tp = lax.axis_index("tp")
    chunks = tokens // chunk

    loads = [pltpu.make_async_copy(w_uk_hbm, w_uk, load_sem.at[0])]
    for c in range(chunks):
        part_of = pl.ds(c * chunk, chunk)
        loads.append(
            pltpu.make_async_copy(
                prefix_hbm.at[:, part_of], cache.at[:, part_of], load_sem.at[1 + c]
            )
        )
    for o in range(own):
        loads.append(
            pltpu.make_async_copy(
                suffix_hbm.at[o],
                cache.at[:, pl.ds(tokens + o * suffix, suffix)],
                load_sem.at[1 + chunks + o],
            )
        )
    first_head = (me * block_rows) // requests
    uv_load = pltpu.make_async_copy(
        w_uv_hbm.at[pl.ds(first_head, block_heads)], w_uv, load_sem.at[1 + chunks + own]
    )
    out_load = pltpu.make_async_copy(w_out_hbm, w_out, load_sem.at[2 + chunks + own])
    for load in loads:
        load.start()
    uv_load.start()
    out_load.start()

    barrier = pltpu.get_barrier_semaphore()
    for k in range(1, n):
        pl.semaphore_signal(
            barrier, inc=1, device_id=(lax.rem(me + k, n), me_tp), device_id_type=MESH
        )
    for k in range(1, t):
        pl.semaphore_signal(
            barrier, inc=1, device_id=(me, lax.rem(me_tp + k, t)), device_id_type=MESH
        )
    pl.semaphore_wait(barrier, n - 1 + t - 1)

    q_copies = []
    for k in range(1, n):
        to = (lax.rem(me + k, n), me_tp)
        for i, (src, dst) in enumerate(((q_nope_ref, qn_all), (q_rope_ref, qr_all))):
            copy = pltpu.make_async_remote_copy(
                src_ref=src,
                dst_ref=dst.at[pl.ds(me * own, own)],
                send_sem=q_send.at[i, k],
                recv_sem=q_recv.at[i, k],
                device_id=to,
                device_id_type=MESH,
            )
            copy.start()
            q_copies.append(copy)
    qn_all[pl.ds(me * own, own)] = q_nope_ref[...]
    qr_all[pl.ds(me * own, own)] = q_rope_ref[...]

    row = lax.broadcasted_iota(jnp.int32, (requests, LANES), 0)
    lane = lax.broadcasted_iota(jnp.int32, (requests, LANES), 1)
    limit = jnp.zeros((requests, LANES), jnp.int32)
    for r in range(requests):
        limit = jnp.where(row == r, prefix_len_ref[r], limit)
    per_tile = LANES // BLOCK
    for i in range(tokens // LANES):
        position = lane + table_ref[i * per_tile] * BLOCK
        for j in range(1, per_tile):
            moved = lane + (table_ref[i * per_tile + j] * BLOCK - j * BLOCK)
            position = jnp.where(lane >= j * BLOCK, moved, position)
        mask[:, i * LANES : (i + 1) * LANES] = jnp.where(position < limit, 0.0, MASKED)
    for o in range(own):
        for i in range(suffix // LANES):
            slot = lane + i * LANES
            start = tokens + o * suffix + i * LANES
            seen = (slot < suffix_len_ref[o]) & (row == me * own + o)
            mask[:, start : start + LANES] = jnp.where(seen, 0.0, MASKED)

    to_row = lax.broadcasted_iota(jnp.int32, (rows, rows), 0)
    from_row = lax.broadcasted_iota(jnp.int32, (rows, rows), 1)
    wanted = (to_row % requests) * heads + to_row // requests
    shuffle = jnp.where(from_row == wanted, 1.0, 0.0).astype(jnp.bfloat16)
    for copy in q_copies:
        copy.wait()
    qn_rows[...] = jnp.dot(
        shuffle, qn_all[...].reshape(rows, NOPE), preferred_element_type=jnp.float32
    )
    query[:, LAT:] = jnp.dot(
        shuffle, qr_all[...].reshape(rows, ROPE), preferred_element_type=jnp.float32
    ).astype(jnp.bfloat16)
    loads[0].wait()
    group = 8

    def absorb(g, carry):
        latents = []
        for j in range(group):
            h = g * group + j
            q = qn_rows[pl.ds(pl.multiple_of(h * requests, requests), requests), :]
            latents.append(
                jnp.dot(q.astype(jnp.bfloat16), w_uk[h], preferred_element_type=jnp.float32)
            )
        at = pl.multiple_of(g * (group * requests), group * requests)
        query[pl.ds(at, group * requests), :LAT] = jnp.concatenate(latents, axis=0).astype(
            jnp.bfloat16
        )
        return carry

    lax.fori_loop(0, heads // group, absorb, 0)

    scale = LOG2E * (NOPE + ROPE) ** (-0.5)
    spans = [(c * chunk, chunk) for c in range(chunks)]
    spans += [(tokens + o * suffix, suffix) for o in range(own)]
    half = n // 2
    side = me // half
    place = lax.rem(me, half)
    part_rows = rows // 2
    m_copies = []
    for turn in range(2):
        part_side = lax.rem(side + 1 + turn, 2)
        base = pl.multiple_of(part_side * part_rows, part_rows)
        for i, (start, length) in enumerate(spans):
            if turn == 0:
                loads[1 + i].wait()
            s = jnp.dot(
                query[pl.ds(base, part_rows), :],
                cache[:, start : start + length],
                preferred_element_type=jnp.float32,
            )
            s = (s * scale).reshape(part_rows // requests, requests, length)
            s = (s + mask[:, start : start + length][None]).reshape(part_rows, length)
            scores[:, start : start + length] = s
            top = s[:, :LANES]
            for j in range(1, length // LANES):
                top = jnp.maximum(top, s[:, j * LANES : (j + 1) * LANES])
            peak[...] = top if i == 0 else jnp.maximum(peak[...], top)
        highest = jnp.maximum(jnp.max(peak[...], axis=1, keepdims=True), FLOOR)
        peak[...] = jnp.broadcast_to(highest, (part_rows, LANES))
        for i, (start, length) in enumerate(spans):
            p = jnp.exp2(scores[:, start : start + length] - peak[:, :1]).astype(jnp.bfloat16)
            wide = p.astype(jnp.float32)
            total = wide[:, :LANES]
            for j in range(1, length // LANES):
                total = total + wide[:, j * LANES : (j + 1) * LANES]
            mass[...] = total if i == 0 else mass[...] + total
            term = lax.dot_general(
                p,
                cache[:LAT, start : start + length],
                (((1,), (1,)), ((), ())),
                preferred_element_type=jnp.float32,
            )
            weighted[...] = term if i == 0 else weighted[...] + term

        sums = jnp.sum(mass[...], axis=1, keepdims=True)
        at_lane = lax.broadcasted_iota(jnp.int32, (part_rows, LANES), 1)
        stats = jnp.zeros((part_rows, LANES), jnp.float32)
        for i, piece in enumerate(thirds(peak[:, :1]) + thirds(sums)):
            stats = jnp.where(at_lane == i, piece, stats)
        slots = pl.ds(part_side * half, half)
        msg[slots, :, :LAT] = weighted[...].astype(jnp.bfloat16).reshape(half, block_rows, LAT)
        msg[slots, :, LAT:] = stats.astype(jnp.bfloat16).reshape(half, block_rows, LANES)
        for k in range(turn, half):
            to = part_side * half + lax.rem(place + k, half)
            slot = turn * half + k
            copy = pltpu.make_async_remote_copy(
                src_ref=msg.at[to],
                dst_ref=got.at[slot],
                send_sem=m_send.at[slot],
                recv_sem=m_recv.at[slot],
                device_id=(to, me_tp),
                device_id_type=MESH,
            )
            copy.start()
            m_copies.append(copy)
    got[half] = msg[me]
    uv_load.wait()
    for copy in m_copies:
        copy.wait()

    tops, totals = [], []
    for k in range(n):
        stat = got[k, :, LAT:].astype(jnp.float32)
        tops.append(stat[:, 0:1] + stat[:, 1:2] + stat[:, 2:3])
        totals.append(stat[:, 3:4] + stat[:, 4:5] + stat[:, 5:6])
    best = functools.reduce(jnp.maximum, tops)
    factors = [jnp.exp2(top - best) for top in tops]
    whole = sum(f * m for f, m in zip(factors, totals))
    latent = sum(f * got[k, :, :LAT].astype(jnp.float32) for k, f in enumerate(factors)) / whole
    values = []
    for j in range(block_heads):
        pieces = jnp.concatenate(thirds(latent[j * head_rows : (j + 1) * head_rows]), axis=0)
        y = jnp.dot(pieces.astype(jnp.bfloat16), w_uv[j], preferred_element_type=jnp.float32)
        values.append(y[:head_rows] + y[head_rows : 2 * head_rows] + y[2 * head_rows :])
    hv_all[me] = jnp.concatenate(values, axis=1).astype(jnp.bfloat16)
    h_copies = []
    for k in range(1, n):
        copy = pltpu.make_async_remote_copy(
            src_ref=hv_all.at[me],
            dst_ref=hv_all.at[me],
            send_sem=h_send.at[k],
            recv_sem=h_recv.at[k],
            device_id=(lax.rem(me + k, n), me_tp),
            device_id_type=MESH,
        )
        copy.start()
        h_copies.append(copy)
    out_load.wait()

    if block_rows >= requests:
        depth = block_heads * vdim
        total = None
        for k in range(n):
            source = lax.rem(me + n - k, n)
            if k:
                h_copies[k - 1].wait_recv()
            term = jnp.dot(
                hv_all[source],
                w_out[pl.ds(pl.multiple_of(source * depth, depth), depth), :],
                preferred_element_type=jnp.float32,
            )
            total = term if k == 0 else total + term
    else:
        for copy in h_copies:
            copy.wait_recv()
        split = requests // block_rows
        total = None
        for h in range(heads):
            lhs = jnp.concatenate([hv_all[h * split + i] for i in range(split)], axis=0)
            term = jnp.dot(
                lhs, w_out[h * vdim : (h + 1) * vdim, :], preferred_element_type=jnp.float32
            )
            total = term if h == 0 else total + term
    for copy in h_copies:
        copy.wait_send()

    share = requests // t
    for i in range(t):
        part[i] = total[i * share : (i + 1) * share]
    p_copies = []
    for k in range(1, t):
        to = lax.rem(me_tp + k, t)
        copy = pltpu.make_async_remote_copy(
            src_ref=part.at[to],
            dst_ref=part_got.at[k],
            send_sem=p_send.at[k],
            recv_sem=p_recv.at[k],
            device_id=(me, to),
            device_id_type=MESH,
        )
        copy.start()
        p_copies.append(copy)
    result = part[me_tp]
    for k in range(1, t):
        p_copies[k - 1].wait()
        result = result + part_got[k]
    out_ref[...] = result.astype(jnp.bfloat16)


def on_device(
    n,
    t,
    q_nope,
    q_rope,
    w_uk,
    w_uv,
    w_out,
    prefix_cache,
    block_table,
    prefix_len,
    suffix_cache,
    suffix_len,
):
    own, heads, _ = q_nope.shape
    requests = own * n
    tokens, width = prefix_cache.shape
    suffix = suffix_cache.shape[1]
    chunk = 1024 if tokens % 1024 == 0 else tokens
    chunks = tokens // chunk
    slots = tokens + own * suffix
    rows = requests * heads
    block_rows = rows // n
    block_heads = max(1, block_rows // requests)
    head_rows = min(block_rows, requests)
    vdim = w_uv.shape[2]
    columns = w_out.shape[1]
    share = requests // t
    bf, f32 = jnp.bfloat16, jnp.float32
    sizes = (n, t, own, heads, requests, tokens, suffix, chunk)
    smem = pl.BlockSpec(memory_space=pltpu.SMEM)
    vmem = pl.BlockSpec(memory_space=pltpu.VMEM)
    hbm = pl.BlockSpec(memory_space=pl.ANY)
    dma = pltpu.SemaphoreType.DMA
    return pl.pallas_call(
        functools.partial(kernel, sizes),
        out_shape=jax.ShapeDtypeStruct((share, columns), bf),
        in_specs=[smem] * 3 + [vmem] * 2 + [hbm] * 5,
        out_specs=vmem,
        scratch_shapes=[
            pltpu.VMEM((requests, heads, NOPE), bf),
            pltpu.VMEM((requests, heads, ROPE), bf),
            pltpu.VMEM((rows, NOPE), f32),
            pltpu.VMEM((rows, width), bf),
            pltpu.VMEM(w_uk.shape, bf),
            pltpu.VMEM((block_heads,) + w_uv.shape[1:], bf),
            pltpu.VMEM(w_out.shape, bf),
            pltpu.VMEM((width, slots), bf),
            pltpu.VMEM((requests, slots), f32),
            pltpu.VMEM((rows // 2, slots), f32),
            pltpu.VMEM((rows // 2, LANES), f32),
            pltpu.VMEM((rows // 2, LANES), f32),
            pltpu.VMEM((rows // 2, LAT), f32),
            pltpu.VMEM((n, block_rows, LAT + LANES), bf),
            pltpu.VMEM((n, block_rows, LAT + LANES), bf),
            pltpu.VMEM((n, head_rows, block_heads * vdim), bf),
            pltpu.VMEM((t, share, columns), f32),
            pltpu.VMEM((t, share, columns), f32),
            dma((3 + chunks + own,)),
            dma((2, n)),
            dma((2, n)),
            dma((n,)),
            dma((n,)),
            dma((n,)),
            dma((n,)),
            dma((t,)),
            dma((t,)),
        ],
        compiler_params=pltpu.CompilerParams(
            collective_id=0, has_side_effects=True, vmem_limit_bytes=60 * 1024 * 1024
        ),
    )(
        block_table,
        prefix_len,
        suffix_len,
        q_nope,
        q_rope,
        w_uk,
        w_uv,
        w_out,
        prefix_cache.T,
        jnp.swapaxes(suffix_cache, 1, 2),
    )


def solution(mesh):
    placed = (
        P("ctx", "tp", None),
        P("ctx", "tp", None),
        P("tp", None, None),
        P("tp", None, None),
        P("tp", "ctx"),
        P("ctx", None),
        P("ctx"),
        P(),
        P("ctx", None, None),
        P("ctx"),
    )
    return jax.shard_map(
        functools.partial(on_device, mesh.shape["ctx"], mesh.shape["tp"]),
        mesh=mesh,
        in_specs=placed,
        out_specs=P("tp", "ctx"),
        check_vma=False,
    )
```

```python
import functools

import jax
import jax.numpy as jnp
from jax import lax
from jax.experimental import pallas as pl
from jax.experimental.pallas import tpu as pltpu
from jax.sharding import PartitionSpec as P

LAT = 512
ROPE = 64
NOPE = 128
BLOCK = 64
LANES = 128
MASKED = -1e30
FLOOR = -1e29
LOG2E = 1.4426950408889634
MESH = pl.DeviceIdType.MESH


def thirds(x):
    a = x.astype(jnp.bfloat16).astype(jnp.float32)
    rest = x - a
    b = rest.astype(jnp.bfloat16).astype(jnp.float32)
    return a, b, (rest - b).astype(jnp.bfloat16).astype(jnp.float32)


def kernel(
    sizes,
    suffix_len_ref,
    table_hbm,
    prefix_len_hbm,
    q_nope_ref,
    q_rope_ref,
    w_uk_hbm,
    w_uv_hbm,
    w_out_hbm,
    prefix_hbm,
    suffix_hbm,
    out_ref,
    qn_all,
    qr_all,
    qn_rows,
    query,
    w_uk,
    w_uv,
    w_out,
    cache,
    mask,
    scores,
    peak,
    mass,
    weighted,
    msg,
    got,
    hv_all,
    part,
    part_got,
    table_ref,
    prefix_len_ref,
    load_sem,
    small_sem,
    q_send,
    q_recv,
    m_send,
    m_recv,
    h_send,
    h_recv,
    p_send,
    p_recv,
):
    n, t, own, heads, requests, tokens, suffix, chunk = sizes
    rows = requests * heads
    block_rows = rows // n
    block_heads = max(1, block_rows // requests)
    head_rows = min(block_rows, requests)
    vdim = w_uv.shape[2]
    me = lax.axis_index("ctx")
    me_tp = lax.axis_index("tp")
    chunks = tokens // chunk

    mine = pl.ds(me * own, own)
    smalls = [
        pltpu.make_async_copy(src, dst, small_sem.at[i])
        for i, (src, dst) in enumerate(
            (
                (table_hbm, table_ref),
                (prefix_len_hbm, prefix_len_ref),
                (q_nope_ref, qn_all.at[mine]),
                (q_rope_ref, qr_all.at[mine]),
            )
        )
    ]
    for small in smalls:
        small.start()
    loads = [pltpu.make_async_copy(w_uk_hbm, w_uk, load_sem.at[0])]
    for c in range(chunks):
        part_of = pl.ds(c * chunk, chunk)
        loads.append(
            pltpu.make_async_copy(
                prefix_hbm.at[:, part_of], cache.at[:, part_of], load_sem.at[1 + c]
            )
        )
    for o in range(own):
        loads.append(
            pltpu.make_async_copy(
                suffix_hbm.at[o],
                cache.at[:, pl.ds(tokens + o * suffix, suffix)],
                load_sem.at[1 + chunks + o],
            )
        )
    first_head = (me * block_rows) // requests
    uv_load = pltpu.make_async_copy(
        w_uv_hbm.at[pl.ds(first_head, block_heads)], w_uv, load_sem.at[1 + chunks + own]
    )
    out_load = pltpu.make_async_copy(w_out_hbm, w_out, load_sem.at[2 + chunks + own])
    barrier = pltpu.get_barrier_semaphore()
    for k in range(1, n):
        pl.semaphore_signal(
            barrier, inc=1, device_id=(lax.rem(me + k, n), me_tp), device_id_type=MESH
        )
    for k in range(1, t):
        pl.semaphore_signal(
            barrier, inc=1, device_id=(me, lax.rem(me_tp + k, t)), device_id_type=MESH
        )
    loads[0].start()
    pl.semaphore_wait(barrier, n - 1 + t - 1)

    q_copies = []
    for k in range(1, n):
        to = (lax.rem(me + k, n), me_tp)
        for i, (src, dst) in enumerate(((q_nope_ref, qn_all), (q_rope_ref, qr_all))):
            copy = pltpu.make_async_remote_copy(
                src_ref=src,
                dst_ref=dst.at[mine],
                send_sem=q_send.at[i, k],
                recv_sem=q_recv.at[i, k],
                device_id=to,
                device_id_type=MESH,
            )
            copy.start()
            q_copies.append(copy)
    for load in loads[1:]:
        load.start()
    uv_load.start()
    out_load.start()
    for small in smalls:
        small.wait()

    row = lax.broadcasted_iota(jnp.int32, (requests, LANES), 0)
    lane = lax.broadcasted_iota(jnp.int32, (requests, LANES), 1)
    limit = jnp.zeros((requests, LANES), jnp.int32)
    for r in range(requests):
        limit = jnp.where(row == r, prefix_len_ref[r], limit)
    per_tile = LANES // BLOCK
    for i in range(tokens // LANES):
        position = lane + table_ref[i * per_tile] * BLOCK
        for j in range(1, per_tile):
            moved = lane + (table_ref[i * per_tile + j] * BLOCK - j * BLOCK)
            position = jnp.where(lane >= j * BLOCK, moved, position)
        mask[:, i * LANES : (i + 1) * LANES] = jnp.where(position < limit, 0.0, MASKED)
    for o in range(own):
        for i in range(suffix // LANES):
            slot = lane + i * LANES
            start = tokens + o * suffix + i * LANES
            seen = (slot < suffix_len_ref[o]) & (row == me * own + o)
            mask[:, start : start + LANES] = jnp.where(seen, 0.0, MASKED)

    to_row = lax.broadcasted_iota(jnp.int32, (rows, rows), 0)
    from_row = lax.broadcasted_iota(jnp.int32, (rows, rows), 1)
    wanted = (to_row % requests) * heads + to_row // requests
    shuffle = jnp.where(from_row == wanted, 1.0, 0.0).astype(jnp.bfloat16)
    for copy in q_copies:
        copy.wait()
    qn_rows[...] = jnp.dot(
        shuffle, qn_all[...].reshape(rows, NOPE), preferred_element_type=jnp.float32
    )
    query[:, LAT:] = jnp.dot(
        shuffle, qr_all[...].reshape(rows, ROPE), preferred_element_type=jnp.float32
    ).astype(jnp.bfloat16)
    loads[0].wait()
    group = 8

    def absorb(g, carry):
        latents = []
        for j in range(group):
            h = g * group + j
            q = qn_rows[pl.ds(pl.multiple_of(h * requests, requests), requests), :]
            latents.append(
                jnp.dot(q.astype(jnp.bfloat16), w_uk[h], preferred_element_type=jnp.float32)
            )
        at = pl.multiple_of(g * (group * requests), group * requests)
        query[pl.ds(at, group * requests), :LAT] = jnp.concatenate(latents, axis=0).astype(
            jnp.bfloat16
        )
        return carry

    lax.fori_loop(0, heads // group, absorb, 0)

    scale = LOG2E * (NOPE + ROPE) ** (-0.5)
    spans = [(c * chunk, chunk) for c in range(chunks)]
    spans += [(tokens + o * suffix, suffix) for o in range(own)]
    half = n // 2
    side = me // half
    place = lax.rem(me, half)
    part_rows = rows // 2
    m_copies = []
    for turn in range(2):
        part_side = lax.rem(side + 1 + turn, 2)
        base = pl.multiple_of(part_side * part_rows, part_rows)
        for i, (start, length) in enumerate(spans):
            if turn == 0:
                loads[1 + i].wait()
            s = jnp.dot(
                query[pl.ds(base, part_rows), :],
                cache[:, start : start + length],
                preferred_element_type=jnp.float32,
            )
            s = (s * scale).reshape(part_rows // requests, requests, length)
            s = (s + mask[:, start : start + length][None]).reshape(part_rows, length)
            scores[:, start : start + length] = s
            top = s[:, :LANES]
            for j in range(1, length // LANES):
                top = jnp.maximum(top, s[:, j * LANES : (j + 1) * LANES])
            peak[...] = top if i == 0 else jnp.maximum(peak[...], top)
        highest = jnp.maximum(jnp.max(peak[...], axis=1, keepdims=True), FLOOR)
        peak[...] = jnp.broadcast_to(highest, (part_rows, LANES))
        for i, (start, length) in enumerate(spans):
            p = jnp.exp2(scores[:, start : start + length] - peak[:, :1]).astype(jnp.bfloat16)
            wide = p.astype(jnp.float32)
            total = wide[:, :LANES]
            for j in range(1, length // LANES):
                total = total + wide[:, j * LANES : (j + 1) * LANES]
            mass[...] = total if i == 0 else mass[...] + total
            term = lax.dot_general(
                p,
                cache[:LAT, start : start + length],
                (((1,), (1,)), ((), ())),
                preferred_element_type=jnp.float32,
            )
            weighted[...] = term if i == 0 else weighted[...] + term

        sums = jnp.sum(mass[...], axis=1, keepdims=True)
        at_lane = lax.broadcasted_iota(jnp.int32, (part_rows, LANES), 1)
        stats = jnp.zeros((part_rows, LANES), jnp.float32)
        for i, piece in enumerate(thirds(peak[:, :1]) + thirds(sums)):
            stats = jnp.where(at_lane == i, piece, stats)
        slots = pl.ds(part_side * half, half)
        msg[slots, :, :LAT] = weighted[...].astype(jnp.bfloat16).reshape(half, block_rows, LAT)
        msg[slots, :, LAT:] = stats.astype(jnp.bfloat16).reshape(half, block_rows, LANES)
        for k in range(turn, half):
            to = part_side * half + lax.rem(place + k, half)
            slot = turn * half + k
            copy = pltpu.make_async_remote_copy(
                src_ref=msg.at[to],
                dst_ref=got.at[slot],
                send_sem=m_send.at[slot],
                recv_sem=m_recv.at[slot],
                device_id=(to, me_tp),
                device_id_type=MESH,
            )
            copy.start()
            m_copies.append(copy)
    got[half] = msg[me]
    uv_load.wait()
    for copy in m_copies:
        copy.wait()

    tops, totals = [], []
    for k in range(n):
        stat = got[k, :, LAT:].astype(jnp.float32)
        tops.append(stat[:, 0:1] + stat[:, 1:2] + stat[:, 2:3])
        totals.append(stat[:, 3:4] + stat[:, 4:5] + stat[:, 5:6])
    best = functools.reduce(jnp.maximum, tops)
    factors = [jnp.exp2(top - best) for top in tops]
    whole = sum(f * m for f, m in zip(factors, totals))
    latent = sum(f * got[k, :, :LAT].astype(jnp.float32) for k, f in enumerate(factors)) / whole
    values = []
    for j in range(block_heads):
        pieces = jnp.concatenate(thirds(latent[j * head_rows : (j + 1) * head_rows]), axis=0)
        y = jnp.dot(pieces.astype(jnp.bfloat16), w_uv[j], preferred_element_type=jnp.float32)
        values.append(y[:head_rows] + y[head_rows : 2 * head_rows] + y[2 * head_rows :])
    hv_all[me] = jnp.concatenate(values, axis=1).astype(jnp.bfloat16)
    h_copies = []
    sources = []
    for turn in range(2):
        to_side = lax.rem(side + 1 + turn, 2)
        for k in range(turn, half):
            copy = pltpu.make_async_remote_copy(
                src_ref=hv_all.at[me],
                dst_ref=hv_all.at[me],
                send_sem=h_send.at[turn * half + k],
                recv_sem=h_recv.at[turn * half + k],
                device_id=(to_side * half + lax.rem(place + k, half), me_tp),
                device_id_type=MESH,
            )
            copy.start()
            h_copies.append(copy)
            sources.append(to_side * half + lax.rem(place + half - k, half))
    out_load.wait()

    if block_rows >= requests:
        depth = block_heads * vdim
        total = None
        for source, copy in [(me, None)] + list(zip(sources, h_copies))[::-1]:
            if copy is not None:
                copy.wait_recv()
            term = jnp.dot(
                hv_all[source],
                w_out[pl.ds(pl.multiple_of(source * depth, depth), depth), :],
                preferred_element_type=jnp.float32,
            )
            total = term if copy is None else total + term
    else:
        for copy in h_copies:
            copy.wait_recv()
        split = requests // block_rows
        total = None
        for h in range(heads):
            lhs = jnp.concatenate([hv_all[h * split + i] for i in range(split)], axis=0)
            term = jnp.dot(
                lhs, w_out[h * vdim : (h + 1) * vdim, :], preferred_element_type=jnp.float32
            )
            total = term if h == 0 else total + term
    for copy in h_copies:
        copy.wait_send()

    share = requests // t
    for i in range(t):
        part[i] = total[i * share : (i + 1) * share]
    p_copies = []
    for k in range(1, t):
        to = lax.rem(me_tp + k, t)
        copy = pltpu.make_async_remote_copy(
            src_ref=part.at[to],
            dst_ref=part_got.at[k],
            send_sem=p_send.at[k],
            recv_sem=p_recv.at[k],
            device_id=(me, to),
            device_id_type=MESH,
        )
        copy.start()
        p_copies.append(copy)
    result = part[me_tp]
    for k in range(1, t):
        p_copies[k - 1].wait()
        result = result + part_got[k]
    out_ref[...] = result.astype(jnp.bfloat16)


def on_device(
    n,
    t,
    q_nope,
    q_rope,
    w_uk,
    w_uv,
    w_out,
    prefix_cache,
    block_table,
    prefix_len,
    suffix_cache,
    suffix_len,
):
    own, heads, _ = q_nope.shape
    requests = own * n
    tokens, width = prefix_cache.shape
    suffix = suffix_cache.shape[1]
    chunk = 2048 if tokens % 2048 == 0 else tokens
    chunks = tokens // chunk
    slots = tokens + own * suffix
    rows = requests * heads
    block_rows = rows // n
    block_heads = max(1, block_rows // requests)
    head_rows = min(block_rows, requests)
    vdim = w_uv.shape[2]
    columns = w_out.shape[1]
    share = requests // t
    bf, f32 = jnp.bfloat16, jnp.float32
    sizes = (n, t, own, heads, requests, tokens, suffix, chunk)
    vmem = pl.BlockSpec(memory_space=pltpu.VMEM)
    hbm = pl.BlockSpec(memory_space=pl.ANY)
    dma = pltpu.SemaphoreType.DMA
    return pl.pallas_call(
        functools.partial(kernel, sizes),
        out_shape=jax.ShapeDtypeStruct((share, columns), bf),
        in_specs=[pl.BlockSpec(memory_space=pltpu.SMEM)] + [hbm] * 9,
        out_specs=vmem,
        scratch_shapes=[
            pltpu.VMEM((requests, heads, NOPE), bf),
            pltpu.VMEM((requests, heads, ROPE), bf),
            pltpu.VMEM((rows, NOPE), f32),
            pltpu.VMEM((rows, width), bf),
            pltpu.VMEM(w_uk.shape, bf),
            pltpu.VMEM((block_heads,) + w_uv.shape[1:], bf),
            pltpu.VMEM(w_out.shape, bf),
            pltpu.VMEM((width, slots), bf),
            pltpu.VMEM((requests, slots), f32),
            pltpu.VMEM((rows // 2, slots), f32),
            pltpu.VMEM((rows // 2, LANES), f32),
            pltpu.VMEM((rows // 2, LANES), f32),
            pltpu.VMEM((rows // 2, LAT), f32),
            pltpu.VMEM((n, block_rows, LAT + LANES), bf),
            pltpu.VMEM((n, block_rows, LAT + LANES), bf),
            pltpu.VMEM((n, head_rows, block_heads * vdim), bf),
            pltpu.VMEM((t, share, columns), f32),
            pltpu.VMEM((t, share, columns), f32),
            pltpu.SMEM(block_table.shape, jnp.int32),
            pltpu.SMEM(prefix_len.shape, jnp.int32),
            dma((3 + chunks + own,)),
            dma((4,)),
            dma((2, n)),
            dma((2, n)),
            dma((n,)),
            dma((n,)),
            dma((n,)),
            dma((n,)),
            dma((t,)),
            dma((t,)),
        ],
        compiler_params=pltpu.CompilerParams(
            collective_id=0, has_side_effects=True, vmem_limit_bytes=60 * 1024 * 1024
        ),
    )(
        suffix_len,
        block_table,
        prefix_len,
        q_nope,
        q_rope,
        w_uk,
        w_uv,
        w_out,
        prefix_cache.T,
        jnp.swapaxes(suffix_cache, 1, 2),
    )


def solution(mesh):
    placed = (
        P("ctx", "tp", None),
        P("ctx", "tp", None),
        P("tp", None, None),
        P("tp", None, None),
        P("tp", "ctx"),
        P("ctx", None),
        P("ctx"),
        P(),
        P("ctx", None, None),
        P("ctx"),
    )
    return jax.shard_map(
        functools.partial(on_device, mesh.shape["ctx"], mesh.shape["tp"]),
        mesh=mesh,
        in_specs=placed,
        out_specs=P("tp", "ctx"),
        check_vma=False,
    )
```

```python
import functools

import jax
import jax.numpy as jnp
from jax import lax
from jax.experimental import pallas as pl
from jax.experimental.pallas import tpu as pltpu
from jax.sharding import PartitionSpec as P

LAT = 512
ROPE = 64
NOPE = 128
BLOCK = 64
LANES = 128
MASKED = -1e30
FLOOR = -1e29
LOG2E = 1.4426950408889634
MESH = pl.DeviceIdType.MESH


def thirds(x):
    a = x.astype(jnp.bfloat16).astype(jnp.float32)
    rest = x - a
    b = rest.astype(jnp.bfloat16).astype(jnp.float32)
    return a, b, (rest - b).astype(jnp.bfloat16).astype(jnp.float32)


def kernel(
    sizes,
    suffix_len_ref,
    table_hbm,
    prefix_len_hbm,
    q_nope_ref,
    q_rope_ref,
    w_uk_hbm,
    w_uv_hbm,
    w_out_hbm,
    prefix_hbm,
    suffix_hbm,
    out_ref,
    qn_all,
    qr_all,
    qn_rows,
    query,
    w_uk,
    w_uv,
    w_out,
    cache,
    mask,
    scores,
    peak,
    mass,
    weighted,
    msg,
    got,
    stat_msg,
    stat_got,
    stat_rows,
    stat_columns,
    hv_all,
    part,
    part_got,
    table_ref,
    prefix_len_ref,
    load_sem,
    small_sem,
    q_send,
    q_recv,
    m_send,
    m_recv,
    s_send,
    s_recv,
    h_send,
    h_recv,
    p_send,
    p_recv,
):
    n, t, own, heads, requests, tokens, suffix, chunk = sizes
    rows = requests * heads
    block_rows = rows // n
    block_heads = max(1, block_rows // requests)
    head_rows = min(block_rows, requests)
    vdim = w_uv.shape[2]
    me = lax.axis_index("ctx")
    me_tp = lax.axis_index("tp")
    chunks = tokens // chunk

    mine = pl.ds(me * own, own)
    smalls = [
        pltpu.make_async_copy(src, dst, small_sem.at[i])
        for i, (src, dst) in enumerate(
            (
                (table_hbm, table_ref),
                (prefix_len_hbm, prefix_len_ref),
                (q_nope_ref, qn_all.at[mine]),
                (q_rope_ref, qr_all.at[mine]),
            )
        )
    ]
    for small in smalls:
        small.start()
    loads = [pltpu.make_async_copy(w_uk_hbm, w_uk, load_sem.at[0])]
    for c in range(chunks):
        part_of = pl.ds(c * chunk, chunk)
        loads.append(
            pltpu.make_async_copy(
                prefix_hbm.at[:, part_of], cache.at[:, part_of], load_sem.at[1 + c]
            )
        )
    for o in range(own):
        loads.append(
            pltpu.make_async_copy(
                suffix_hbm.at[o],
                cache.at[:, pl.ds(tokens + o * suffix, suffix)],
                load_sem.at[1 + chunks + o],
            )
        )
    first_head = (me * block_rows) // requests
    uv_load = pltpu.make_async_copy(
        w_uv_hbm.at[pl.ds(first_head, block_heads)], w_uv, load_sem.at[1 + chunks + own]
    )
    out_load = pltpu.make_async_copy(w_out_hbm, w_out, load_sem.at[2 + chunks + own])
    barrier = pltpu.get_barrier_semaphore()
    for k in range(1, n):
        pl.semaphore_signal(
            barrier, inc=1, device_id=(lax.rem(me + k, n), me_tp), device_id_type=MESH
        )
    for k in range(1, t):
        pl.semaphore_signal(
            barrier, inc=1, device_id=(me, lax.rem(me_tp + k, t)), device_id_type=MESH
        )
    loads[0].start()
    pl.semaphore_wait(barrier, n - 1 + t - 1)

    q_copies = []
    for k in range(1, n):
        to = (lax.rem(me + k, n), me_tp)
        for i, (src, dst) in enumerate(((q_nope_ref, qn_all), (q_rope_ref, qr_all))):
            copy = pltpu.make_async_remote_copy(
                src_ref=src,
                dst_ref=dst.at[mine],
                send_sem=q_send.at[i, k],
                recv_sem=q_recv.at[i, k],
                device_id=to,
                device_id_type=MESH,
            )
            copy.start()
            q_copies.append(copy)
    for load in loads[1:]:
        load.start()
    uv_load.start()
    out_load.start()
    for small in smalls:
        small.wait()

    stat_rows[...] = jnp.zeros_like(stat_rows)

    row = lax.broadcasted_iota(jnp.int32, (requests, LANES), 0)
    lane = lax.broadcasted_iota(jnp.int32, (requests, LANES), 1)
    limit = jnp.zeros((requests, LANES), jnp.int32)
    for r in range(requests):
        limit = jnp.where(row == r, prefix_len_ref[r], limit)
    per_tile = LANES // BLOCK
    for i in range(tokens // LANES):
        position = lane + table_ref[i * per_tile] * BLOCK
        for j in range(1, per_tile):
            moved = lane + (table_ref[i * per_tile + j] * BLOCK - j * BLOCK)
            position = jnp.where(lane >= j * BLOCK, moved, position)
        mask[:, i * LANES : (i + 1) * LANES] = jnp.where(position < limit, 0.0, MASKED)
    for o in range(own):
        for i in range(suffix // LANES):
            slot = lane + i * LANES
            start = tokens + o * suffix + i * LANES
            seen = (slot < suffix_len_ref[o]) & (row == me * own + o)
            mask[:, start : start + LANES] = jnp.where(seen, 0.0, MASKED)

    to_row = lax.broadcasted_iota(jnp.int32, (rows, rows), 0)
    from_row = lax.broadcasted_iota(jnp.int32, (rows, rows), 1)
    wanted = (to_row % requests) * heads + to_row // requests
    shuffle = jnp.where(from_row == wanted, 1.0, 0.0).astype(jnp.bfloat16)
    for copy in q_copies:
        copy.wait()
    qn_rows[...] = jnp.dot(
        shuffle, qn_all[...].reshape(rows, NOPE), preferred_element_type=jnp.float32
    )
    query[:, LAT:] = jnp.dot(
        shuffle, qr_all[...].reshape(rows, ROPE), preferred_element_type=jnp.float32
    ).astype(jnp.bfloat16)
    loads[0].wait()
    group = 8

    def absorb(g, carry):
        latents = []
        for j in range(group):
            h = g * group + j
            q = qn_rows[pl.ds(pl.multiple_of(h * requests, requests), requests), :]
            latents.append(
                jnp.dot(q.astype(jnp.bfloat16), w_uk[h], preferred_element_type=jnp.float32)
            )
        at = pl.multiple_of(g * (group * requests), group * requests)
        query[pl.ds(at, group * requests), :LAT] = jnp.concatenate(latents, axis=0).astype(
            jnp.bfloat16
        )
        return carry

    lax.fori_loop(0, heads // group, absorb, 0)

    scale = LOG2E * (NOPE + ROPE) ** (-0.5)
    spans = [(c * chunk, chunk) for c in range(chunks)]
    spans += [(tokens + o * suffix, suffix) for o in range(own)]
    half = n // 2
    side = me // half
    place = lax.rem(me, half)
    part_rows = rows // 2
    m_copies = []
    for turn in range(2):
        part_side = lax.rem(side + 1 + turn, 2)
        base = pl.multiple_of(part_side * part_rows, part_rows)
        for i, (start, length) in enumerate(spans):
            if turn == 0:
                loads[1 + i].wait()
            s = jnp.dot(
                query[pl.ds(base, part_rows), :],
                cache[:, start : start + length],
                preferred_element_type=jnp.float32,
            )
            s = (s * scale).reshape(part_rows // requests, requests, length)
            s = (s + mask[:, start : start + length][None]).reshape(part_rows, length)
            scores[:, start : start + length] = s
            top = s[:, :LANES]
            for j in range(1, length // LANES):
                top = jnp.maximum(top, s[:, j * LANES : (j + 1) * LANES])
            peak[...] = top if i == 0 else jnp.maximum(peak[...], top)
        highest = jnp.maximum(jnp.max(peak[...], axis=1, keepdims=True), FLOOR)
        peak[...] = jnp.broadcast_to(highest, (part_rows, LANES))
        for i, (start, length) in enumerate(spans):
            p = jnp.exp2(scores[:, start : start + length] - peak[:, :1]).astype(jnp.bfloat16)
            wide = p.astype(jnp.float32)
            total = wide[:, :LANES]
            for j in range(1, length // LANES):
                total = total + wide[:, j * LANES : (j + 1) * LANES]
            mass[...] = total if i == 0 else mass[...] + total
            term = lax.dot_general(
                p,
                cache[:LAT, start : start + length],
                (((1,), (1,)), ((), ())),
                preferred_element_type=jnp.float32,
            )
            weighted[...] = term if i == 0 else weighted[...] + term

        sums = jnp.sum(mass[...], axis=1, keepdims=True)
        at_lane = lax.broadcasted_iota(jnp.int32, (part_rows, LANES), 1)
        stats = jnp.where(at_lane == 0, peak[...], sums)
        stat_msg[turn] = jnp.transpose(stats)[:2]
        slots = pl.ds(part_side * half, half)
        msg[slots] = weighted[...].astype(jnp.bfloat16).reshape(half, block_rows, LAT)
        for k in range(turn, half):
            to = part_side * half + lax.rem(place + k, half)
            slot = turn * half + k
            copy = pltpu.make_async_remote_copy(
                src_ref=msg.at[to],
                dst_ref=got.at[slot],
                send_sem=m_send.at[slot],
                recv_sem=m_recv.at[slot],
                device_id=(to, me_tp),
                device_id_type=MESH,
            )
            copy.start()
            m_copies.append(copy)
            copy = pltpu.make_async_remote_copy(
                src_ref=stat_msg.at[turn],
                dst_ref=stat_got.at[slot],
                send_sem=s_send.at[slot],
                recv_sem=s_recv.at[slot],
                device_id=(to, me_tp),
                device_id_type=MESH,
            )
            copy.start()
            m_copies.append(copy)
    got[half] = msg[me]
    stat_got[half] = stat_msg[1]
    uv_load.wait()
    for copy in m_copies:
        copy.wait()

    for k in range(n):
        stat_rows[2 * k : 2 * k + 2, :] = stat_got[k]
    stat_columns[...] = jnp.transpose(stat_rows[...])
    stat = stat_columns[pl.ds(pl.multiple_of(place * block_rows, block_rows), block_rows), :]
    tops = [stat[:, 2 * k : 2 * k + 1] for k in range(n)]
    totals = [stat[:, 2 * k + 1 : 2 * k + 2] for k in range(n)]
    best = functools.reduce(jnp.maximum, tops)
    factors = [jnp.exp2(top - best) for top in tops]
    whole = sum(f * m for f, m in zip(factors, totals))
    latent = sum(f * got[k].astype(jnp.float32) for k, f in enumerate(factors)) / whole
    values = []
    for j in range(block_heads):
        pieces = jnp.concatenate(thirds(latent[j * head_rows : (j + 1) * head_rows]), axis=0)
        y = jnp.dot(pieces.astype(jnp.bfloat16), w_uv[j], preferred_element_type=jnp.float32)
        values.append(y[:head_rows] + y[head_rows : 2 * head_rows] + y[2 * head_rows :])
    hv_all[me] = jnp.concatenate(values, axis=1).astype(jnp.bfloat16)
    h_copies = []
    sources = []
    for turn in range(2):
        to_side = lax.rem(side + 1 + turn, 2)
        for k in range(turn, half):
            copy = pltpu.make_async_remote_copy(
                src_ref=hv_all.at[me],
                dst_ref=hv_all.at[me],
                send_sem=h_send.at[turn * half + k],
                recv_sem=h_recv.at[turn * half + k],
                device_id=(to_side * half + lax.rem(place + k, half), me_tp),
                device_id_type=MESH,
            )
            copy.start()
            h_copies.append(copy)
            sources.append(to_side * half + lax.rem(place + half - k, half))
    out_load.wait()

    if block_rows >= requests:
        depth = block_heads * vdim
        total = None
        for source, copy in [(me, None)] + list(zip(sources, h_copies))[::-1]:
            if copy is not None:
                copy.wait_recv()
            term = jnp.dot(
                hv_all[source],
                w_out[pl.ds(pl.multiple_of(source * depth, depth), depth), :],
                preferred_element_type=jnp.float32,
            )
            total = term if copy is None else total + term
    else:
        for copy in h_copies:
            copy.wait_recv()
        split = requests // block_rows
        total = None
        for h in range(heads):
            lhs = jnp.concatenate([hv_all[h * split + i] for i in range(split)], axis=0)
            term = jnp.dot(
                lhs, w_out[h * vdim : (h + 1) * vdim, :], preferred_element_type=jnp.float32
            )
            total = term if h == 0 else total + term
    for copy in h_copies:
        copy.wait_send()

    share = requests // t
    for i in range(t):
        part[i] = total[i * share : (i + 1) * share]
    p_copies = []
    for k in range(1, t):
        to = lax.rem(me_tp + k, t)
        copy = pltpu.make_async_remote_copy(
            src_ref=part.at[to],
            dst_ref=part_got.at[k],
            send_sem=p_send.at[k],
            recv_sem=p_recv.at[k],
            device_id=(me, to),
            device_id_type=MESH,
        )
        copy.start()
        p_copies.append(copy)
    result = part[me_tp]
    for k in range(1, t):
        p_copies[k - 1].wait()
        result = result + part_got[k]
    out_ref[...] = result.astype(jnp.bfloat16)


def on_device(
    n,
    t,
    q_nope,
    q_rope,
    w_uk,
    w_uv,
    w_out,
    prefix_cache,
    block_table,
    prefix_len,
    suffix_cache,
    suffix_len,
):
    own, heads, _ = q_nope.shape
    requests = own * n
    tokens, width = prefix_cache.shape
    suffix = suffix_cache.shape[1]
    chunk = 2048 if tokens % 2048 == 0 else tokens
    chunks = tokens // chunk
    slots = tokens + own * suffix
    rows = requests * heads
    block_rows = rows // n
    block_heads = max(1, block_rows // requests)
    head_rows = min(block_rows, requests)
    vdim = w_uv.shape[2]
    columns = w_out.shape[1]
    share = requests // t
    bf, f32 = jnp.bfloat16, jnp.float32
    sizes = (n, t, own, heads, requests, tokens, suffix, chunk)
    vmem = pl.BlockSpec(memory_space=pltpu.VMEM)
    hbm = pl.BlockSpec(memory_space=pl.ANY)
    dma = pltpu.SemaphoreType.DMA
    return pl.pallas_call(
        functools.partial(kernel, sizes),
        out_shape=jax.ShapeDtypeStruct((share, columns), bf),
        in_specs=[pl.BlockSpec(memory_space=pltpu.SMEM)] + [hbm] * 9,
        out_specs=vmem,
        scratch_shapes=[
            pltpu.VMEM((requests, heads, NOPE), bf),
            pltpu.VMEM((requests, heads, ROPE), bf),
            pltpu.VMEM((rows, NOPE), f32),
            pltpu.VMEM((rows, width), bf),
            pltpu.VMEM(w_uk.shape, bf),
            pltpu.VMEM((block_heads,) + w_uv.shape[1:], bf),
            pltpu.VMEM(w_out.shape, bf),
            pltpu.VMEM((width, slots), bf),
            pltpu.VMEM((requests, slots), f32),
            pltpu.VMEM((rows // 2, slots), f32),
            pltpu.VMEM((rows // 2, LANES), f32),
            pltpu.VMEM((rows // 2, LANES), f32),
            pltpu.VMEM((rows // 2, LAT), f32),
            pltpu.VMEM((n, block_rows, LAT), bf),
            pltpu.VMEM((n, block_rows, LAT), bf),
            pltpu.VMEM((2, 2, rows // 2), f32),
            pltpu.VMEM((n, 2, rows // 2), f32),
            pltpu.VMEM((LANES, rows // 2), f32),
            pltpu.VMEM((rows // 2, LANES), f32),
            pltpu.VMEM((n, head_rows, block_heads * vdim), bf),
            pltpu.VMEM((t, share, columns), f32),
            pltpu.VMEM((t, share, columns), f32),
            pltpu.SMEM(block_table.shape, jnp.int32),
            pltpu.SMEM(prefix_len.shape, jnp.int32),
            dma((3 + chunks + own,)),
            dma((4,)),
            dma((2, n)),
            dma((2, n)),
            dma((n,)),
            dma((n,)),
            dma((n,)),
            dma((n,)),
            dma((n,)),
            dma((n,)),
            dma((t,)),
            dma((t,)),
        ],
        compiler_params=pltpu.CompilerParams(
            collective_id=0, has_side_effects=True, vmem_limit_bytes=60 * 1024 * 1024
        ),
    )(
        suffix_len,
        block_table,
        prefix_len,
        q_nope,
        q_rope,
        w_uk,
        w_uv,
        w_out,
        prefix_cache.T,
        jnp.swapaxes(suffix_cache, 1, 2),
    )


def solution(mesh):
    placed = (
        P("ctx", "tp", None),
        P("ctx", "tp", None),
        P("tp", None, None),
        P("tp", None, None),
        P("tp", "ctx"),
        P("ctx", None),
        P("ctx"),
        P(),
        P("ctx", None, None),
        P("ctx"),
    )
    return jax.shard_map(
        functools.partial(on_device, mesh.shape["ctx"], mesh.shape["tp"]),
        mesh=mesh,
        in_specs=placed,
        out_specs=P("tp", "ctx"),
        check_vma=False,
    )
```

```python
import functools

import jax
import jax.numpy as jnp
from jax import lax
from jax.experimental import pallas as pl
from jax.experimental.pallas import tpu as pltpu
from jax.sharding import PartitionSpec as P

LAT = 512
ROPE = 64
NOPE = 128
BLOCK = 64
LANES = 128
MASKED = -1e30
FLOOR = -1e29
LOG2E = 1.4426950408889634
MESH = pl.DeviceIdType.MESH


def thirds(x):
    a = x.astype(jnp.bfloat16).astype(jnp.float32)
    rest = x - a
    b = rest.astype(jnp.bfloat16).astype(jnp.float32)
    return a, b, (rest - b).astype(jnp.bfloat16).astype(jnp.float32)


def kernel(
    sizes,
    suffix_len_ref,
    table_hbm,
    prefix_len_hbm,
    q_nope_ref,
    q_rope_ref,
    w_uk_hbm,
    w_uv_hbm,
    w_out_hbm,
    prefix_hbm,
    suffix_hbm,
    out_ref,
    qn_all,
    qr_all,
    qn_rows,
    query,
    w_uk,
    w_uv,
    w_out,
    cache,
    mask,
    scores,
    peak,
    mass,
    weighted,
    msg,
    got,
    stat_msg,
    stat_got,
    stat_rows,
    stat_columns,
    hv_all,
    part,
    part_got,
    table_ref,
    prefix_len_ref,
    load_sem,
    small_sem,
    q_send,
    q_recv,
    m_send,
    m_recv,
    s_send,
    s_recv,
    h_send,
    h_recv,
    p_send,
    p_recv,
):
    n, t, own, heads, requests, tokens, suffix, chunk = sizes
    rows = requests * heads
    block_rows = rows // n
    block_heads = max(1, block_rows // requests)
    head_rows = min(block_rows, requests)
    vdim = w_uv.shape[2]
    me = lax.axis_index("ctx")
    me_tp = lax.axis_index("tp")
    chunks = tokens // chunk

    mine = pl.ds(me * own, own)
    smalls = [
        pltpu.make_async_copy(src, dst, small_sem.at[i])
        for i, (src, dst) in enumerate(
            (
                (table_hbm, table_ref),
                (prefix_len_hbm, prefix_len_ref),
                (q_nope_ref, qn_all.at[mine]),
                (q_rope_ref, qr_all.at[mine]),
            )
        )
    ]
    for small in smalls:
        small.start()
    loads = [pltpu.make_async_copy(w_uk_hbm, w_uk, load_sem.at[0])]
    for c in range(chunks):
        part_of = pl.ds(c * chunk, chunk)
        loads.append(
            pltpu.make_async_copy(
                prefix_hbm.at[:, part_of], cache.at[:, part_of], load_sem.at[1 + c]
            )
        )
    for o in range(own):
        loads.append(
            pltpu.make_async_copy(
                suffix_hbm.at[o],
                cache.at[:, pl.ds(tokens + o * suffix, suffix)],
                load_sem.at[1 + chunks + o],
            )
        )
    first_head = (me * block_rows) // requests
    uv_load = pltpu.make_async_copy(
        w_uv_hbm.at[pl.ds(first_head, block_heads)], w_uv, load_sem.at[1 + chunks + own]
    )
    out_load = pltpu.make_async_copy(w_out_hbm, w_out, load_sem.at[2 + chunks + own])
    barrier = pltpu.get_barrier_semaphore()
    for k in range(1, n):
        pl.semaphore_signal(
            barrier, inc=1, device_id=(lax.rem(me + k, n), me_tp), device_id_type=MESH
        )
    for k in range(1, t):
        pl.semaphore_signal(
            barrier, inc=1, device_id=(me, lax.rem(me_tp + k, t)), device_id_type=MESH
        )
    loads[0].start()
    pl.semaphore_wait(barrier, n - 1 + t - 1)

    q_copies = []
    for k in range(1, n):
        to = (lax.rem(me + k, n), me_tp)
        for i, (src, dst) in enumerate(((q_nope_ref, qn_all), (q_rope_ref, qr_all))):
            copy = pltpu.make_async_remote_copy(
                src_ref=src,
                dst_ref=dst.at[mine],
                send_sem=q_send.at[i, k],
                recv_sem=q_recv.at[i, k],
                device_id=to,
                device_id_type=MESH,
            )
            copy.start()
            q_copies.append(copy)
    for load in loads[1:]:
        load.start()
    uv_load.start()
    out_load.start()
    for small in smalls:
        small.wait()

    stat_rows[...] = jnp.zeros_like(stat_rows)

    row = lax.broadcasted_iota(jnp.int32, (requests, LANES), 0)
    lane = lax.broadcasted_iota(jnp.int32, (requests, LANES), 1)
    limit = jnp.zeros((requests, LANES), jnp.int32)
    for r in range(requests):
        limit = jnp.where(row == r, prefix_len_ref[r], limit)
    per_tile = LANES // BLOCK
    for i in range(tokens // LANES):
        position = lane + table_ref[i * per_tile] * BLOCK
        for j in range(1, per_tile):
            moved = lane + (table_ref[i * per_tile + j] * BLOCK - j * BLOCK)
            position = jnp.where(lane >= j * BLOCK, moved, position)
        mask[:, i * LANES : (i + 1) * LANES] = jnp.where(position < limit, 0.0, MASKED)
    for o in range(own):
        for i in range(suffix // LANES):
            slot = lane + i * LANES
            start = tokens + o * suffix + i * LANES
            seen = (slot < suffix_len_ref[o]) & (row == me * own + o)
            mask[:, start : start + LANES] = jnp.where(seen, 0.0, MASKED)

    to_row = lax.broadcasted_iota(jnp.int32, (rows, rows), 0)
    from_row = lax.broadcasted_iota(jnp.int32, (rows, rows), 1)
    wanted = (to_row % requests) * heads + to_row // requests
    shuffle = jnp.where(from_row == wanted, 1.0, 0.0).astype(jnp.bfloat16)
    for copy in q_copies:
        copy.wait()
    qn_rows[...] = jnp.dot(
        shuffle, qn_all[...].reshape(rows, NOPE), preferred_element_type=jnp.float32
    )
    query[:, LAT:] = jnp.dot(
        shuffle, qr_all[...].reshape(rows, ROPE), preferred_element_type=jnp.float32
    ).astype(jnp.bfloat16)
    loads[0].wait()
    group = heads

    def absorb(g, carry):
        latents = []
        for j in range(group):
            h = g * group + j
            q = qn_rows[pl.ds(pl.multiple_of(h * requests, requests), requests), :]
            latents.append(
                jnp.dot(q.astype(jnp.bfloat16), w_uk[h], preferred_element_type=jnp.float32)
            )
        at = pl.multiple_of(g * (group * requests), group * requests)
        query[pl.ds(at, group * requests), :LAT] = jnp.concatenate(latents, axis=0).astype(
            jnp.bfloat16
        )
        return carry

    lax.fori_loop(0, heads // group, absorb, 0)

    scale = LOG2E * (NOPE + ROPE) ** (-0.5)
    spans = [(c * chunk, chunk) for c in range(chunks)]
    spans += [(tokens + o * suffix, suffix) for o in range(own)]
    half = n // 2
    side = me // half
    place = lax.rem(me, half)
    part_rows = rows // 2
    m_copies = []
    for turn in range(2):
        part_side = lax.rem(side + 1 + turn, 2)
        base = pl.multiple_of(part_side * part_rows, part_rows)
        for i, (start, length) in enumerate(spans):
            if turn == 0:
                loads[1 + i].wait()
            s = jnp.dot(
                query[pl.ds(base, part_rows), :],
                cache[:, start : start + length],
                preferred_element_type=jnp.float32,
            )
            s = (s * scale).reshape(part_rows // requests, requests, length)
            s = (s + mask[:, start : start + length][None]).reshape(part_rows, length)
            scores[turn, :, start : start + length] = s
            top = s[:, :LANES]
            for j in range(1, length // LANES):
                top = jnp.maximum(top, s[:, j * LANES : (j + 1) * LANES])
            peak[turn] = top if i == 0 else jnp.maximum(peak[turn], top)
        highest = jnp.maximum(jnp.max(peak[turn], axis=1, keepdims=True), FLOOR)
        peak[turn] = jnp.broadcast_to(highest, (part_rows, LANES))
        for i, (start, length) in enumerate(spans):
            p = jnp.exp2(scores[turn, :, start : start + length] - peak[turn, :, :1]).astype(jnp.bfloat16)
            wide = p.astype(jnp.float32)
            total = wide[:, :LANES]
            for j in range(1, length // LANES):
                total = total + wide[:, j * LANES : (j + 1) * LANES]
            mass[turn] = total if i == 0 else mass[turn] + total
            term = lax.dot_general(
                p,
                cache[:LAT, start : start + length],
                (((1,), (1,)), ((), ())),
                preferred_element_type=jnp.float32,
            )
            weighted[turn] = term if i == 0 else weighted[turn] + term

        sums = jnp.sum(mass[turn], axis=1, keepdims=True)
        at_lane = lax.broadcasted_iota(jnp.int32, (part_rows, LANES), 1)
        stats = jnp.where(at_lane == 0, peak[turn], sums)
        stat_msg[turn] = jnp.transpose(stats)[:2]
        slots = pl.ds(part_side * half, half)
        msg[slots] = weighted[turn].astype(jnp.bfloat16).reshape(half, block_rows, LAT)
        for k in range(turn, half):
            to = part_side * half + lax.rem(place + k, half)
            slot = turn * half + k
            copy = pltpu.make_async_remote_copy(
                src_ref=msg.at[to],
                dst_ref=got.at[slot],
                send_sem=m_send.at[slot],
                recv_sem=m_recv.at[slot],
                device_id=(to, me_tp),
                device_id_type=MESH,
            )
            copy.start()
            m_copies.append(copy)
            copy = pltpu.make_async_remote_copy(
                src_ref=stat_msg.at[turn],
                dst_ref=stat_got.at[slot],
                send_sem=s_send.at[slot],
                recv_sem=s_recv.at[slot],
                device_id=(to, me_tp),
                device_id_type=MESH,
            )
            copy.start()
            m_copies.append(copy)
    got[half] = msg[me]
    stat_got[half] = stat_msg[1]
    uv_load.wait()
    for copy in m_copies:
        copy.wait()

    for k in range(n):
        stat_rows[2 * k : 2 * k + 2, :] = stat_got[k]
    stat_columns[...] = jnp.transpose(stat_rows[...])
    stat = stat_columns[pl.ds(pl.multiple_of(place * block_rows, block_rows), block_rows), :]
    tops = [stat[:, 2 * k : 2 * k + 1] for k in range(n)]
    totals = [stat[:, 2 * k + 1 : 2 * k + 2] for k in range(n)]
    best = functools.reduce(jnp.maximum, tops)
    factors = [jnp.exp2(top - best) for top in tops]
    whole = sum(f * m for f, m in zip(factors, totals))
    latent = sum(f * got[k].astype(jnp.float32) for k, f in enumerate(factors)) / whole
    values = []
    for j in range(block_heads):
        pieces = jnp.concatenate(thirds(latent[j * head_rows : (j + 1) * head_rows]), axis=0)
        y = jnp.dot(pieces.astype(jnp.bfloat16), w_uv[j], preferred_element_type=jnp.float32)
        values.append(y[:head_rows] + y[head_rows : 2 * head_rows] + y[2 * head_rows :])
    hv_all[me] = jnp.concatenate(values, axis=1).astype(jnp.bfloat16)
    h_copies = []
    sources = []
    for turn in range(2):
        to_side = lax.rem(side + 1 + turn, 2)
        for k in range(turn, half):
            copy = pltpu.make_async_remote_copy(
                src_ref=hv_all.at[me],
                dst_ref=hv_all.at[me],
                send_sem=h_send.at[turn * half + k],
                recv_sem=h_recv.at[turn * half + k],
                device_id=(to_side * half + lax.rem(place + k, half), me_tp),
                device_id_type=MESH,
            )
            copy.start()
            h_copies.append(copy)
            sources.append(to_side * half + lax.rem(place + half - k, half))
    out_load.wait()

    if block_rows >= requests:
        depth = block_heads * vdim
        total = None
        for source, copy in [(me, None)] + list(zip(sources, h_copies))[::-1]:
            if copy is not None:
                copy.wait_recv()
            term = jnp.dot(
                hv_all[source],
                w_out[pl.ds(pl.multiple_of(source * depth, depth), depth), :],
                preferred_element_type=jnp.float32,
            )
            total = term if copy is None else total + term
    else:
        for copy in h_copies:
            copy.wait_recv()
        split = requests // block_rows
        total = None
        for h in range(heads):
            lhs = jnp.concatenate([hv_all[h * split + i] for i in range(split)], axis=0)
            term = jnp.dot(
                lhs, w_out[h * vdim : (h + 1) * vdim, :], preferred_element_type=jnp.float32
            )
            total = term if h == 0 else total + term
    share = requests // t
    for i in range(t):
        part[i] = total[i * share : (i + 1) * share]
    p_copies = []
    for k in range(1, t):
        to = lax.rem(me_tp + k, t)
        copy = pltpu.make_async_remote_copy(
            src_ref=part.at[to],
            dst_ref=part_got.at[k],
            send_sem=p_send.at[k],
            recv_sem=p_recv.at[k],
            device_id=(me, to),
            device_id_type=MESH,
        )
        copy.start()
        p_copies.append(copy)
    for copy in h_copies:
        copy.wait_send()
    result = part[me_tp]
    for k in range(1, t):
        p_copies[k - 1].wait()
        result = result + part_got[k]
    out_ref[...] = result.astype(jnp.bfloat16)


def on_device(
    n,
    t,
    q_nope,
    q_rope,
    w_uk,
    w_uv,
    w_out,
    prefix_cache,
    block_table,
    prefix_len,
    suffix_cache,
    suffix_len,
):
    own, heads, _ = q_nope.shape
    requests = own * n
    tokens, width = prefix_cache.shape
    suffix = suffix_cache.shape[1]
    chunk = 4096 if tokens % 4096 == 0 else tokens
    chunks = tokens // chunk
    slots = tokens + own * suffix
    rows = requests * heads
    block_rows = rows // n
    block_heads = max(1, block_rows // requests)
    head_rows = min(block_rows, requests)
    vdim = w_uv.shape[2]
    columns = w_out.shape[1]
    share = requests // t
    bf, f32 = jnp.bfloat16, jnp.float32
    sizes = (n, t, own, heads, requests, tokens, suffix, chunk)
    vmem = pl.BlockSpec(memory_space=pltpu.VMEM)
    hbm = pl.BlockSpec(memory_space=pl.ANY)
    dma = pltpu.SemaphoreType.DMA
    return pl.pallas_call(
        functools.partial(kernel, sizes),
        out_shape=jax.ShapeDtypeStruct((share, columns), bf),
        in_specs=[pl.BlockSpec(memory_space=pltpu.SMEM)] + [hbm] * 9,
        out_specs=vmem,
        scratch_shapes=[
            pltpu.VMEM((requests, heads, NOPE), bf),
            pltpu.VMEM((requests, heads, ROPE), bf),
            pltpu.VMEM((rows, NOPE), f32),
            pltpu.VMEM((rows, width), bf),
            pltpu.VMEM(w_uk.shape, bf),
            pltpu.VMEM((block_heads,) + w_uv.shape[1:], bf),
            pltpu.VMEM(w_out.shape, bf),
            pltpu.VMEM((width, slots), bf),
            pltpu.VMEM((requests, slots), f32),
            pltpu.VMEM((2, rows // 2, slots), f32),
            pltpu.VMEM((2, rows // 2, LANES), f32),
            pltpu.VMEM((2, rows // 2, LANES), f32),
            pltpu.VMEM((2, rows // 2, LAT), f32),
            pltpu.VMEM((n, block_rows, LAT), bf),
            pltpu.VMEM((n, block_rows, LAT), bf),
            pltpu.VMEM((2, 2, rows // 2), f32),
            pltpu.VMEM((n, 2, rows // 2), f32),
            pltpu.VMEM((LANES, rows // 2), f32),
            pltpu.VMEM((rows // 2, LANES), f32),
            pltpu.VMEM((n, head_rows, block_heads * vdim), bf),
            pltpu.VMEM((t, share, columns), f32),
            pltpu.VMEM((t, share, columns), f32),
            pltpu.SMEM(block_table.shape, jnp.int32),
            pltpu.SMEM(prefix_len.shape, jnp.int32),
            dma((3 + chunks + own,)),
            dma((4,)),
            dma((2, n)),
            dma((2, n)),
            dma((n,)),
            dma((n,)),
            dma((n,)),
            dma((n,)),
            dma((n,)),
            dma((n,)),
            dma((t,)),
            dma((t,)),
        ],
        compiler_params=pltpu.CompilerParams(
            collective_id=0, has_side_effects=True, vmem_limit_bytes=60 * 1024 * 1024
        ),
    )(
        suffix_len,
        block_table,
        prefix_len,
        q_nope,
        q_rope,
        w_uk,
        w_uv,
        w_out,
        prefix_cache.T,
        jnp.swapaxes(suffix_cache, 1, 2),
    )


def solution(mesh):
    placed = (
        P("ctx", "tp", None),
        P("ctx", "tp", None),
        P("tp", None, None),
        P("tp", None, None),
        P("tp", "ctx"),
        P("ctx", None),
        P("ctx"),
        P(),
        P("ctx", None, None),
        P("ctx"),
    )
    return jax.shard_map(
        functools.partial(on_device, mesh.shape["ctx"], mesh.shape["tp"]),
        mesh=mesh,
        in_specs=placed,
        out_specs=P("tp", "ctx"),
        check_vma=False,
    )
```
